512 devices in a mesh: layer: 32 (over x, z_lo, core), row: 4 (over y), col: 4 (over z_hi).
Axes of the slice: x: 4, y: 4, z: 16 (z_hi: 4, z_lo: 4; z = z_hi * 4 + z_lo), core: 2. Of those that a mesh axis runs over, the one named last changes fastest.
Arguments:
- reflect_fwd: float32 [32, 1024, 1024], P('layer', 'row', 'col'), may hold values from -1 to 1
- transmit_fwd: float32 [32, 1024, 1024], P('layer', 'row', 'col'), may hold values from -1 to 1
- reflect_bwd: float32 [32, 1024, 1024], P('layer', 'row', 'col'), may hold values from -1 to 1
- transmit_bwd: float32 [32, 1024, 1024], P('layer', 'row', 'col'), may hold values from -1 to 1
- material_ids: int32 [32], P('layer'), may hold values from 0 to 7
- interface_gain: float32 [8, 1024], replicated, may hold values from 0.5 to 1
Outputs:
- reflect_out: float32 [32, 1024, 1024], P('layer', 'row', 'col')
- transmit_out: float32 [32, 1024, 1024], P('layer', 'row', 'col')
The draws below stay inside these ranges and needn't reach their ends.
All inputs are finite; a program needn't handle non-finite values.
Results may differ from the reference program's by a relative error of at most 0.00015.
Values sent between devices are 32-bit elements; how exact they have to be, the bound alone decides.
A program may use at most 64 MiB of HBM per device.

```python
import math
import jax
import jax.numpy as jnp
from jax import lax

NTERMS = 6
NMAT = 8
M = 1024
NCOMP = 32
N_LAYER = 32


def operator_draw(key, low_diag, high_diag, spread):
    noise_key, diag_key = jax.random.split(key)
    shape_full = (N_LAYER, M, M)
    diagonal_mask = (lax.broadcasted_iota(jnp.int32, shape_full, 1) == lax.broadcasted_iota(jnp.int32, shape_full, 2)).astype(jnp.float32)
    noise = jax.random.normal(noise_key, shape_full, jnp.float32) * (spread / math.sqrt(M))
    diag_values = jax.random.uniform(diag_key, (N_LAYER, M, 1), jnp.float32, low_diag, high_diag)
    noise = jnp.clip(noise, -0.2, 0.2)
    return noise * (1.0 - diagonal_mask) + diagonal_mask * diag_values


def draw_reflect_fwd(key, part):
    return operator_draw(jax.random.fold_in(key, 11), 0.5, 0.8, 0.15)


def draw_transmit_fwd(key, part):
    return operator_draw(jax.random.fold_in(key, 23), 0.3, 0.6, 0.12)


def draw_reflect_bwd(key, part):
    return operator_draw(jax.random.fold_in(key, 37), 0.5, 0.8, 0.15)


def draw_transmit_bwd(key, part):
    return operator_draw(jax.random.fold_in(key, 41), 0.3, 0.6, 0.12)


def touch_ends(values, key, low, largest):
    longest = values.shape.index(max(values.shape))
    spots = []
    for shift in (0, 1):
        where = [jax.random.randint(jax.random.fold_in(key, axis), (), 0, length) for axis, length in enumerate(values.shape)]
        where[longest] = (where[longest] + shift) % values.shape[longest]
        spots.append(tuple(where))
    return values.at[spots[0]].set(low).at[spots[1]].set(largest)


def setup_inputs(seed: int = 0) -> dict:
    splits = jax.random.split(jax.random.key(seed), 7)
    reflect_fwd = draw_reflect_fwd(jax.random.fold_in(splits[6], 71), 0)
    transmit_fwd = draw_transmit_fwd(jax.random.fold_in(splits[6], 71), 0)
    reflect_bwd = draw_reflect_bwd(jax.random.fold_in(splits[6], 71), 0)
    transmit_bwd = draw_transmit_bwd(jax.random.fold_in(splits[6], 71), 0)
    material_ids = touch_ends(jax.random.randint(splits[4], (NCOMP,), 0, NMAT), jax.random.fold_in(splits[4], 1), 0, NMAT - 1).astype(jnp.int32)
    interface_gain = jnp.clip(jax.random.uniform(splits[5], (NMAT, M), jnp.float32, 0.5, 1.0), 0.5, 1.0)
    return {"reflect_fwd": reflect_fwd, "transmit_fwd": transmit_fwd, "reflect_bwd": reflect_bwd, "transmit_bwd": transmit_bwd, "material_ids": material_ids, "interface_gain": interface_gain}


def product(left, right):
    return jnp.dot(left, right, precision=lax.Precision.HIGHEST)


def pair_product(reflect_a, transmit_a, reflect_back_a, transmit_back_a, reflect_b, transmit_b, weight):
    scaled_fwd = weight[:, None] * transmit_a
    scaled_bwd = transmit_back_a * weight[None, :]
    power_term = product(reflect_back_a, reflect_b)
    side_term = product(scaled_bwd, reflect_b)
    identity = jnp.eye(M, dtype=reflect_a.dtype)
    series = identity + power_term
    for repeat in range(NTERMS - 2):
        series = identity + product(power_term, series)
    middle = product(series, scaled_fwd)
    return reflect_a + product(side_term, middle), product(transmit_b, middle)


def reference(reflect_fwd, transmit_fwd, reflect_bwd, transmit_bwd, material_ids, interface_gain):
    distance = N_LAYER // 2
    gain_rows = interface_gain[material_ids]
    weights = gain_rows[:distance] * gain_rows[distance:]

    def single(operands):
        return pair_product(*operands)

    reflect_pair, transmit_pair = lax.map(single, (reflect_fwd[:distance], transmit_fwd[:distance], reflect_bwd[:distance], transmit_bwd[:distance], reflect_fwd[distance:], transmit_fwd[distance:], weights))
    reflect_out = jnp.concatenate([reflect_pair, reflect_pair], axis=0)
    transmit_out = jnp.concatenate([transmit_pair, transmit_pair], axis=0)
    return (reflect_out, transmit_out)
```

```python
import jax
import jax.numpy as jnp
from jax import lax
from jax.experimental import pallas as pl
from jax.experimental.pallas import tpu as pltpu
from jax.sharding import PartitionSpec as P

NTERMS = 6
MESH = pl.DeviceIdType.MESH
F32 = jnp.float32
BF16 = jnp.bfloat16
ORDER = (0, 3, 1, 2)

Z_RB, Z_TB, Z_RF, Z_TF, Z_FT, Z_WA, Z_WB = 0, 1, 2, 3, 4, 8, 9
R_RB, R_TB, R_TF, R_SS, R_RF, R_MT, R_PA, R_PB = 10, 14, 18, 22, 26, 30, 34, 38
C_RF, C_MT, C_PP = 54, 58, 62
O_PRIM, O_SEC, O_RA = 78, 80, 82
N_RECV = 83
N_SEND = 120

NN = (((1,), (0,)), ((), ()))
NT = (((1,), (1,)), ((), ()))


def split(value):
    high = value.astype(BF16)
    low = (value - high.astype(F32)).astype(BF16)
    return high, low


def dot3(left, right, dims):
    lh, ll = left
    rh, rl = right

    def one(a, b):
        return lax.dot_general(a, b, dims, preferred_element_type=F32)

    return one(lh, rh) + (one(lh, rl) + one(ll, rh))


def kernel(rf_ref, tf_ref, rb_ref, tb_ref, mid_ref, gain_ref,
           prim_ref, sec_ref, ra_ref,
           rb, tb, tf, ss, rf, pp, ph, plo, ft, mt, ot, ob, own_gain, wa, wb, fts,
           ssem, rsem):
    lay = lax.axis_index("layer")
    y = lax.axis_index("row")
    zh = lax.axis_index("col")
    x = lay // 8
    zl = lax.rem(lay // 2, 4)
    c = lax.rem(lay, 2)
    z = zh * 4 + zl
    blk = rf_ref.shape[0]
    half = blk // 2
    quarter = half // 2
    wide = rf.shape[0]
    fine = ft.shape[0]

    upper = x < 2
    zp = lax.rem(zl + 2 + 4 * (2 * lax.rem(x, 2) + c), 16)
    zhp = zp // 4
    zlp = lax.rem(zp, 4)

    def plane(yd, cd):
        return (zh * 8 + zlp * 2 + cd, yd, zhp)

    zz = lax.rem(z + 14, 16)
    sq = zz // 4
    src_lay = (sq // 2) * 8 + lax.rem(zz, 4) * 2 + lax.rem(sq, 2)

    def source(lower, yd):
        return (src_lay + 16 * lower, yd, x)

    def near(xd, yd):
        return (lax.rem(xd, 4) * 8 + zl * 2 + c, lax.rem(yd, 4), zh)

    cross = (lay + 1 - 2 * c, y, zh)
    partner = (lax.rem(lay + 16, 32), y, zh)

    barrier = pltpu.get_barrier_semaphore()

    def signal(device):
        pl.semaphore_signal(barrier, inc=1, device_id=device, device_id_type=MESH)

    for yd in range(4):
        signal(source(0, yd))
    signal(source(1, y))
    for cd in range(2):
        signal(plane(y, cd))
    signal(near(x + 1, y))
    signal(near(x + 3, y))
    signal(near(x, y + 1))
    signal(near(x, y + 3))
    signal(cross)
    signal(partner)

    rows8 = lax.broadcasted_iota(jnp.int32, gain_ref.shape, 0)
    own = jnp.sum(jnp.where(rows8 == mid_ref[0], gain_ref[...], 0.0), axis=0, keepdims=True)
    own_gain[...] = jnp.broadcast_to(own, own_gain.shape)
    fts[...] = tf_ref[...].T

    @pl.when(upper)
    def _():
        pl.semaphore_wait(barrier, 16)

    @pl.when(jnp.logical_not(upper))
    def _():
        pl.semaphore_wait(barrier, 10)

    sends = []
    count = [0]

    def copy_of(src, dst, slot, recv, device):
        return pltpu.make_async_remote_copy(
            src_ref=src, dst_ref=dst, send_sem=ssem.at[slot], recv_sem=rsem.at[recv],
            device_id=device, device_id_type=MESH)

    def send(src, dst, recv, device):
        copy = copy_of(src, dst, count[0], recv, device)
        count[0] += 1
        copy.start()
        sends.append(copy)

    def arrived(dst, recv):
        copy_of(dst, dst, 0, recv, cross).wait_recv()

    def al(index, size):
        return pl.ds(pl.multiple_of(index, size), size)

    mine = al(zh * blk, blk)
    ycols = al(y * blk, blk)

    def upper_moves():
        moves = []
        for cd in range(2):
            moves.append((rb_ref.at[pl.ds(cd * half, half), :], rb.at[:, mine], Z_RB, plane(y, cd)))
        for cd in range(2):
            moves.append((own_gain, wa, Z_WA, plane(y, cd)))
        for yd in range(4):
            for cd in range(2):
                moves.append((fts.at[pl.ds((2 * yd + cd) * fine, fine), :], ft.at[:, ycols], Z_FT + y, plane(yd, cd)))
        for cd in range(2):
            moves.append((tb_ref.at[pl.ds(cd * half, half), :], tb.at[:, mine], Z_TB, plane(y, cd)))
        moves.append((rf_ref, ra_ref, O_RA, partner))
        return moves

    def lower_moves():
        moves = []
        for cd in range(2):
            moves.append((rf_ref.at[pl.ds(cd * half, half), :], rf.at[al((2 * y + cd) * half, half), :], Z_RF, plane(y, cd)))
        for cd in range(2):
            moves.append((own_gain, wb, Z_WB, plane(y, cd)))
        for cd in range(2):
            moves.append((tf_ref.at[pl.ds(cd * half, half), :], tf.at[:, mine], Z_TF, plane(y, cd)))
        return moves

    @pl.when(upper)
    def _():
        for slot, (src, dst, recv, device) in enumerate(upper_moves()):
            copy_of(src, dst, slot, recv, device).start()

    @pl.when(jnp.logical_not(upper))
    def _():
        for slot, (src, dst, recv, device) in enumerate(lower_moves()):
            copy_of(src, dst, slot, recv, device).start()

    count[0] = len(upper_moves())

    class Ring:
        def __init__(self, part, me, device, base):
            self.part, self.me, self.device, self.base = part, me, device, base

        def pos(self, step):
            return lax.rem(self.me + step, 4)

        def start(self):
            piece = self.part(self.me, None)
            send(piece, piece, self.base, self.device(self.me + 1))
            send(piece, piece, self.base + 1, self.device(self.me + 3))

        def left(self):
            arrived(self.part(self.pos(3), None), self.base)
            piece = self.part(self.pos(3), 0)
            send(piece, piece, self.base + 2, self.device(self.me + 1))

        def right(self):
            arrived(self.part(self.pos(1), None), self.base + 1)
            piece = self.part(self.pos(1), 1)
            send(piece, piece, self.base + 3, self.device(self.me + 3))

        def far(self):
            arrived(self.part(self.pos(2), 0), self.base + 2)
            arrived(self.part(self.pos(2), 1), self.base + 3)

    def on_x(a):
        return near(a, y)

    def on_y(a):
        return near(x, a)

    def col_part(buf):
        def part(p, h):
            rows = pl.ds(0, half) if h is None else pl.ds(h * quarter, quarter)
            return buf.at[rows, al(p * blk, blk)]
        return part

    def row_part(buf, size, core):
        def part(p, h):
            start = (2 * p + core) * size
            if h is None:
                return buf.at[al(start, size), :]
            return buf.at[al(start + h * (size // 2), size // 2), :]
        return part

    def cross_send(piece, recv):
        send(piece, piece, recv, cross)

    def cross_wait(part, base):
        for k, step in enumerate(ORDER):
            arrived(part(lax.rem(y + step, 4), None), base + k)

    def y_gather(buf, size, base, cbase):
        part = row_part(buf, size, c)
        ring = Ring(part, y, on_y, base)
        ring.start()
        cross_send(part(y, None), cbase)
        yield
        ring.left()
        cross_send(part(ring.pos(3), None), cbase + 1)
        ring.right()
        cross_send(part(ring.pos(1), None), cbase + 2)
        yield
        ring.far()
        cross_send(part(ring.pos(2), None), cbase + 3)
        cross_wait(row_part(buf, size, 1 - c), cbase)
        yield

    rb_ring = Ring(col_part(rb), x, on_x, R_RB)
    tb_ring = Ring(col_part(tb), x, on_x, R_TB)
    tf_ring = Ring(col_part(tf), x, on_x, R_TF)
    ss_ring = Ring(col_part(ss), x, on_x, R_SS)

    arrived(rb.at[:, al(x * blk, blk)], Z_RB)
    rb_ring.start()
    arrived(rf.at[al((2 * y + c) * half, half), :], Z_RF)
    gather = y_gather(rf, half, R_RF, C_RF)
    next(gather)
    rb_ring.left()
    rb_ring.right()
    next(gather)
    rb_ring.far()
    next(gather)
    right = split(rf[...])
    power = dot3(split(rb[...]), right, NN)

    def mix(a, b, core):
        return a + core * (b - a), b + core * (a - b)

    me_a, me_b = mix(x, y, c)

    def ppart(a, b, h, core):
        jj, ii = mix(a, b, core)
        start = (2 * ii + core) * half
        cols = al(jj * blk, blk)
        if h is None:
            return pp.at[al(start, half), cols]
        return pp.at[al(start + h * quarter, quarter), cols]

    def device_ab(a, b):
        return near(*mix(a, b, c))

    pp[al((2 * y + c) * half, half), al(x * blk, blk)] = power
    ring_a = Ring(lambda p, h: ppart(p, me_b, h, c), me_a, lambda a: device_ab(a, me_b), R_PA)
    rings_b = []
    for k, step in enumerate(ORDER):
        a = lax.rem(me_a + step, 4)
        rings_b.append(Ring(
            lambda p, h, a=a: ppart(a, p, h, c), me_b, lambda b: device_ab(me_a, b), R_PB + 4 * k))

    def start_b(k):
        rings_b[k].start()
        cross_send(rings_b[k].part(me_b, None), C_PP + 4 * k)

    def sides_b(k):
        rings_b[k].left()
        cross_send(rings_b[k].part(rings_b[k].pos(3), None), C_PP + 4 * k + 1)
        rings_b[k].right()
        cross_send(rings_b[k].part(rings_b[k].pos(1), None), C_PP + 4 * k + 2)

    def far_b(k):
        rings_b[k].far()
        cross_send(rings_b[k].part(rings_b[k].pos(2), None), C_PP + 4 * k + 3)

    ring_a.start()
    start_b(0)
    ring_a.left()
    start_b(1)
    ring_a.right()
    start_b(2)
    ring_a.far()
    start_b(3)
    sides_b(0)
    sides_b(1)
    arrived(tb.at[:, al(x * blk, blk)], Z_TB)
    tb_ring.start()
    sides_b(2)
    far_b(0)
    far_b(1)
    sides_b(3)
    arrived(tf.at[:, al(x * blk, blk)], Z_TF)
    tf_ring.start()
    tb_ring.left()
    tb_ring.right()
    far_b(2)
    far_b(3)
    tf_ring.left()
    tf_ring.right()
    tb_ring.far()
    arrived(wa, Z_WA)
    arrived(wb, Z_WB)
    weight = wa[...][0:1, :] * wb[...][0:1, :]
    ss[:, al(x * blk, blk)] = dot3(split(tb[...] * weight), right, NN)
    ss_ring.start()
    oa, obb = mix(x, y, 1 - c)
    for k, step in enumerate(ORDER):
        for m, other in enumerate(ORDER):
            arrived(ppart(lax.rem(oa + step, 4), lax.rem(obb + other, 4), None, 1 - c), C_PP + 4 * k + m)
    for yd in range(4):
        arrived(ft.at[:, pl.ds(yd * blk, blk)], Z_FT + yd)
    ph[...], plo[...] = split(pp[...])
    first = ft[...] * weight

    def horner(step, value):
        return first + dot3(split(value), (ph[...], plo[...]), NT)

    value = lax.fori_loop(0, 2, horner, first)
    ss_ring.left()
    ss_ring.right()
    tf_ring.far()
    value = lax.fori_loop(0, NTERMS - 3, horner, value)
    mt[al((2 * y + c) * fine, fine), :] = value
    gather = y_gather(mt, fine, R_MT, C_MT)
    next(gather)
    ss_ring.far()
    next(gather)
    next(gather)

    middle = split(mt[...])
    ot[...] = dot3(split(tf[...]), middle, NT)
    place = al(c * half, half)
    send(ot, prim_ref.at[place, :], O_PRIM + c, source(1, y))
    ob[...] = dot3(split(ss[...]), middle, NT)
    send(ob, prim_ref.at[place, :], O_PRIM + c, source(0, y))

    for h in range(2):
        piece = prim_ref.at[pl.ds(h * half, half), :]
        arrived(piece, O_PRIM + h)
        send(piece, sec_ref.at[pl.ds(h * half, half), :], O_SEC + h, partner)
    for h in range(2):
        arrived(sec_ref.at[pl.ds(h * half, half), :], O_SEC + h)

    @pl.when(upper)
    def _():
        for slot, (src, dst, recv, device) in enumerate(upper_moves()):
            copy_of(src, dst, slot, recv, device).wait_send()

    @pl.when(jnp.logical_not(upper))
    def _():
        for slot, (src, dst, recv, device) in enumerate(lower_moves()):
            copy_of(src, dst, slot, recv, device).wait_send()
        arrived(ra_ref, O_RA)

    for copy in sends:
        copy.wait_send()
    assert count[0] <= N_SEND


def on_device(reflect_fwd, transmit_fwd, reflect_bwd, transmit_bwd, material_ids, interface_gain):
    blk = reflect_fwd.shape[1]
    order = interface_gain.shape[1]
    half = blk // 2
    fine = order // 32
    anywhere = pl.BlockSpec(memory_space=pl.ANY)
    vmem = pl.BlockSpec(memory_space=pltpu.VMEM)
    shape = jax.ShapeDtypeStruct((blk, blk), F32)
    reflect_own = reflect_fwd[0]
    prim, sec, reflect_peer = pl.pallas_call(
        kernel,
        out_shape=(shape, shape, shape),
        in_specs=[anywhere, vmem, anywhere, anywhere, pl.BlockSpec(memory_space=pltpu.SMEM), vmem],
        out_specs=(anywhere, anywhere, anywhere),
        scratch_shapes=[
            pltpu.VMEM((half, order), F32),
            pltpu.VMEM((half, order), F32),
            pltpu.VMEM((half, order), F32),
            pltpu.VMEM((half, order), F32),
            pltpu.VMEM((order, blk), F32),
            pltpu.VMEM((order, order), F32),
            pltpu.VMEM((order, order), BF16),
            pltpu.VMEM((order, order), BF16),
            pltpu.VMEM((fine, order), F32),
            pltpu.VMEM((blk, order), F32),
            pltpu.VMEM((half, blk), F32),
            pltpu.VMEM((half, blk), F32),
            pltpu.VMEM((8, order), F32),
            pltpu.VMEM((8, order), F32),
            pltpu.VMEM((8, order), F32),
            pltpu.VMEM((blk, blk), F32),
            pltpu.SemaphoreType.DMA((N_SEND,)),
            pltpu.SemaphoreType.DMA((N_RECV,)),
        ],
        compiler_params=pltpu.CompilerParams(
            collective_id=0, has_side_effects=True, vmem_limit_bytes=48 * 1024 * 1024),
        name="star",
    )(reflect_own, transmit_fwd[0], reflect_bwd[0], transmit_bwd[0], material_ids, interface_gain)
    upper = lax.axis_index("layer") < lax.axis_size("layer") // 2
    reflect_a = jnp.where(upper, reflect_own, reflect_peer)
    refl_out = reflect_a + jnp.where(upper, prim, sec)
    trans_out = jnp.where(upper, sec, prim)
    return (refl_out[None], trans_out[None])


def solution(mesh):
    placed = (
        P("layer", "row", "col"),
        P("layer", "row", "col"),
        P("layer", "row", "col"),
        P("layer", "row", "col"),
        P("layer"),
        P(),
    )
    return jax.shard_map(
        on_device,
        mesh=mesh,
        in_specs=placed,
        out_specs=(P("layer", "row", "col"), P("layer", "row", "col")),
        check_vma=False,
    )
```

```python
import jax
import jax.numpy as jnp
from jax import lax
from jax.experimental import pallas as pl
from jax.experimental.pallas import tpu as pltpu
from jax.sharding import PartitionSpec as P

NTERMS = 6
MESH = pl.DeviceIdType.MESH
F32 = jnp.float32
BF16 = jnp.bfloat16
ORDER = (0, 3, 1, 2)

PLANE = (13, 10, 2, 4, 8, 1, 14, 6, 11, 3, 7, 12, 5, 15, 9, 0)
SHIFT = (0, 3, 3, 0, 3, 3, 0, 2, 1, 2, 1, 2, 1, 2, 0, 0)

Z_RB, Z_TB, Z_RF, Z_TF, Z_FT, Z_TR, Z_WA, Z_WB = 0, 1, 2, 3, 4, 5, 8, 9
R_RB, R_TB, R_TF, R_SS, R_RF, R_MT, R_PA, R_PB = 10, 14, 18, 22, 26, 30, 34, 38
C_RF, C_MT, C_PP = 54, 58, 62
O_PRIM, O_SEC, O_RA = 78, 80, 82
R_FT = 83
N_RECV = 87
N_SEND = 120

NN = (((1,), (0,)), ((), ()))
NT = (((1,), (1,)), ((), ()))


def split(value):
    high = value.astype(BF16)
    low = (value - high.astype(F32)).astype(BF16)
    return high, low


def dot3(left, right, dims):
    lh, ll = left
    rh, rl = right

    def one(a, b):
        return lax.dot_general(a, b, dims, preferred_element_type=F32)

    return one(lh, rh) + (one(lh, rl) + one(ll, rh))


def lookup(table, index):
    value = jnp.int32(table[0])
    for k in range(1, len(table)):
        value = jnp.where(index == k, jnp.int32(table[k]), value)
    return value


def kernel(rf_ref, tf_ref, rb_ref, tb_ref, mid_ref, gain_ref,
           prim_ref, sec_ref, ra_ref,
           rb, tb, tf, ss, rf, pp, ph, plo, ft, mt, ot, ob, own_gain, wa, wb, fts,
           fv, fr, tr, ssem, rsem, lsem):
    lay = lax.axis_index("layer")
    y = lax.axis_index("row")
    zh = lax.axis_index("col")
    x = lay // 8
    zl = lax.rem(lay // 2, 4)
    c = lax.rem(lay, 2)
    z = zh * 4 + zl
    blk = rf_ref.shape[0]
    half = blk // 2
    quarter = half // 2
    wide = rf.shape[0]
    fine = ft.shape[0]

    upper = lay < 16
    pair = lax.rem(lay, 16)
    zp = lookup(PLANE, pair)
    zhp = zp // 4
    zlp = lax.rem(zp, 4)
    xp = lax.rem(zh + 4 - lookup(SHIFT, pair), 4)

    def plane(cd):
        return (xp * 8 + zlp * 2 + cd, y, zhp)

    task = lookup([PLANE.index(k) for k in range(16)], z)
    shift = lookup(SHIFT, task)
    j = lax.rem(x + shift, 4)

    def source(lower):
        return (task + 16 * lower, y, j)

    def near(jd, yd):
        return (lax.rem(jd + 4 - shift, 4) * 8 + zl * 2 + c, lax.rem(yd, 4), zh)

    cross = (lay + 1 - 2 * c, y, zh)
    partner = (lax.rem(lay + 16, 32), y, zh)

    barrier = pltpu.get_barrier_semaphore()

    def signal(device):
        pl.semaphore_signal(barrier, inc=1, device_id=device, device_id_type=MESH)

    for device in (source(0), source(1), plane(0), plane(1), partner):
        signal(device)
    for step in (1, 3):
        signal(near(j + step, y))
    for step in (1, 2, 3):
        signal(near(j, y + step))
    signal(cross)
    load = pltpu.make_async_copy(tf_ref, fv, lsem)
    load.start()

    rows8 = lax.broadcasted_iota(jnp.int32, gain_ref.shape, 0)
    own = jnp.sum(jnp.where(rows8 == mid_ref[0], gain_ref[...], 0.0), axis=0, keepdims=True)
    own_gain[...] = jnp.broadcast_to(own, own_gain.shape)
    load.wait()
    fts[...] = fv[...].T
    pl.semaphore_wait(barrier, 11)

    sends = []
    count = [0]

    def copy_of(src, dst, slot, recv, device):
        return pltpu.make_async_remote_copy(
            src_ref=src, dst_ref=dst, send_sem=ssem.at[slot], recv_sem=rsem.at[recv],
            device_id=device, device_id_type=MESH)

    def send(src, dst, recv, device):
        copy = copy_of(src, dst, count[0], recv, device)
        count[0] += 1
        copy.start()
        sends.append(copy)

    def arrived(dst, recv):
        copy_of(dst, dst, 0, recv, cross).wait_recv()

    def al(index, size):
        return pl.ds(pl.multiple_of(index, size), size)

    mine = al(zh * blk, blk)
    halves = [pl.ds(0, half), pl.ds(half, half)]

    def upper_moves():
        moves = [(tb_ref.at[halves[1], :], tr, Z_TR, partner)]
        for cd in range(2):
            moves.append((rb_ref.at[halves[cd], :], rb.at[:, mine], Z_RB, plane(cd)))
        for cd in range(2):
            moves.append((own_gain, wa, Z_WA, plane(cd)))
        for cd in range(2):
            moves.append((fts.at[halves[cd], :], fr, Z_FT, plane(cd)))
        moves.append((tb_ref.at[halves[0], :], tb.at[:, mine], Z_TB, plane(0)))
        moves.append((rf_ref, ra_ref, O_RA, partner))
        return moves

    def lower_moves():
        moves = []
        for cd in range(2):
            moves.append((rf_ref.at[halves[cd], :], rf.at[al((2 * y + cd) * half, half), :], Z_RF, plane(cd)))
        for cd in range(2):
            moves.append((own_gain, wb, Z_WB, plane(cd)))
        moves.append((tr, tb.at[:, mine], Z_TB, plane(1)))
        for cd in range(2):
            moves.append((tf_ref.at[halves[cd], :], tf.at[:, mine], Z_TF, plane(cd)))
        return moves

    @pl.when(upper)
    def _():
        for slot, (src, dst, recv, device) in enumerate(upper_moves()):
            copy_of(src, dst, slot, recv, device).start()

    @pl.when(jnp.logical_not(upper))
    def _():
        for slot, (src, dst, recv, device) in enumerate(lower_moves()):
            if recv == Z_TB:
                arrived(tr, Z_TR)
            copy_of(src, dst, slot, recv, device).start()

    count[0] = len(upper_moves())

    class Ring:
        def __init__(self, part, me, device, base):
            self.part, self.me, self.device, self.base = part, me, device, base

        def pos(self, step):
            return lax.rem(self.me + step, 4)

        def start(self):
            piece = self.part(self.me, None)
            send(piece, piece, self.base, self.device(self.me + 1))
            send(piece, piece, self.base + 1, self.device(self.me + 3))

        def left(self):
            arrived(self.part(self.pos(3), None), self.base)
            piece = self.part(self.pos(3), 0)
            send(piece, piece, self.base + 2, self.device(self.me + 1))

        def right(self):
            arrived(self.part(self.pos(1), None), self.base + 1)
            piece = self.part(self.pos(1), 1)
            send(piece, piece, self.base + 3, self.device(self.me + 3))

        def far(self):
            arrived(self.part(self.pos(2), 0), self.base + 2)
            arrived(self.part(self.pos(2), 1), self.base + 3)

    def on_x(a):
        return near(a, y)

    def on_y(a):
        return near(j, a)

    def col_part(buf):
        def part(p, h):
            rows = pl.ds(0, half) if h is None else pl.ds(h * quarter, quarter)
            return buf.at[rows, al(p * blk, blk)]
        return part

    def row_part(buf, size, base):
        def part(p, h):
            start = base(p)
            if h is None:
                return buf.at[al(start, size), :]
            return buf.at[al(start + h * (size // 2), size // 2), :]
        return part

    def cross_send(piece, recv):
        send(piece, piece, recv, cross)

    def cross_wait(part, base):
        for k, step in enumerate(ORDER):
            arrived(part(lax.rem(y + step, 4), None), base + k)

    def y_gather(buf, size, place, base, cbase):
        part = row_part(buf, size, lambda p: place(p, c))
        ring = Ring(part, y, on_y, base)
        ring.start()
        cross_send(part(y, None), cbase)
        yield
        ring.left()
        cross_send(part(ring.pos(3), None), cbase + 1)
        ring.right()
        cross_send(part(ring.pos(1), None), cbase + 2)
        yield
        ring.far()
        cross_send(part(ring.pos(2), None), cbase + 3)
        cross_wait(row_part(buf, size, lambda p: place(p, 1 - c)), cbase)
        yield

    rb_ring = Ring(col_part(rb), j, on_x, R_RB)
    tb_ring = Ring(col_part(tb), j, on_x, R_TB)
    tf_ring = Ring(col_part(tf), j, on_x, R_TF)
    ss_ring = Ring(col_part(ss), j, on_x, R_SS)

    arrived(rb.at[:, al(j * blk, blk)], Z_RB)
    rb_ring.start()
    arrived(rf.at[al((2 * y + c) * half, half), :], Z_RF)
    def rf_place(p, core):
        return (2 * p + core) * half

    def mt_place(p, core):
        return (4 * core + p) * fine

    gather = y_gather(rf, half, rf_place, R_RF, C_RF)
    next(gather)
    rb_ring.left()
    rb_ring.right()
    next(gather)
    rb_ring.far()
    next(gather)
    right = split(rf[...])
    power = dot3(split(rb[...]), right, NN)

    def mix(a, b, core):
        return a + core * (b - a), b + core * (a - b)

    me_a, me_b = mix(j, y, c)

    def ppart(a, b, h, core):
        jj, ii = mix(a, b, core)
        start = (2 * ii + core) * half
        cols = al(jj * blk, blk)
        if h is None:
            return pp.at[al(start, half), cols]
        return pp.at[al(start + h * quarter, quarter), cols]

    def device_ab(a, b):
        return near(*mix(a, b, c))

    pp[al((2 * y + c) * half, half), al(j * blk, blk)] = power
    ring_a = Ring(lambda p, h: ppart(p, me_b, h, c), me_a, lambda a: device_ab(a, me_b), R_PA)
    rings_b = []
    for k, step in enumerate(ORDER):
        a = lax.rem(me_a + step, 4)
        rings_b.append(Ring(
            lambda p, h, a=a: ppart(a, p, h, c), me_b, lambda b: device_ab(me_a, b), R_PB + 4 * k))

    def start_b(k):
        rings_b[k].start()
        cross_send(rings_b[k].part(me_b, None), C_PP + 4 * k)

    def sides_b(k):
        rings_b[k].left()
        cross_send(rings_b[k].part(rings_b[k].pos(3), None), C_PP + 4 * k + 1)
        rings_b[k].right()
        cross_send(rings_b[k].part(rings_b[k].pos(1), None), C_PP + 4 * k + 2)

    def far_b(k):
        rings_b[k].far()
        cross_send(rings_b[k].part(rings_b[k].pos(2), None), C_PP + 4 * k + 3)

    ring_a.start()
    start_b(0)
    ring_a.left()
    start_b(1)
    ring_a.right()
    start_b(2)
    sides_b(0)
    ring_a.far()
    start_b(3)
    sides_b(1)
    sides_b(2)
    far_b(0)
    arrived(fr, Z_FT)
    ycols = al(y * blk, blk)
    for step in (1, 2, 3):
        to = lax.rem(y + step, 4)
        send(fr.at[al(to * fine, fine), :], ft.at[:, ycols], R_FT + y, on_y(to))
    ft[:, ycols] = fr[al(y * fine, fine), :]
    sides_b(3)
    far_b(1)
    far_b(2)
    far_b(3)
    arrived(wa, Z_WA)
    arrived(wb, Z_WB)
    weight = wa[...][0:1, :] * wb[...][0:1, :]
    for step in (1, 2, 3):
        away = lax.rem(y + step, 4)
        arrived(ft.at[:, al(away * blk, blk)], R_FT + away)
    oa, obb = mix(j, y, 1 - c)
    for k, step in enumerate(ORDER):
        for m, other in enumerate(ORDER):
            arrived(ppart(lax.rem(oa + step, 4), lax.rem(obb + other, 4), None, 1 - c), C_PP + 4 * k + m)
    arrived(tb.at[:, al(j * blk, blk)], Z_TB)
    tb_ring.start()
    arrived(tf.at[:, al(j * blk, blk)], Z_TF)
    tf_ring.start()
    ph[...], plo[...] = split(pp[...])
    first = ft[...] * weight

    def horner(step, value):
        return first + dot3(split(value), (ph[...], plo[...]), NT)

    value = lax.fori_loop(0, 2, horner, first)
    tb_ring.left()
    tb_ring.right()
    value = lax.fori_loop(0, NTERMS - 3, horner, value)
    mt[al(mt_place(y, c), fine), :] = value
    gather = y_gather(mt, fine, mt_place, R_MT, C_MT)
    next(gather)
    tb_ring.far()
    ss[:, al(j * blk, blk)] = dot3(split(tb[...] * weight), right, NN)
    ss_ring.start()
    tf_ring.left()
    tf_ring.right()
    next(gather)
    ss_ring.left()
    ss_ring.right()
    tf_ring.far()
    next(gather)

    middle = split(mt[...])
    ot[...] = dot3(split(tf[...]), middle, NT)
    place = al(c * half, half)
    send(ot, prim_ref.at[place, :], O_PRIM + c, source(1))
    ss_ring.far()
    ob[...] = dot3(split(ss[...]), middle, NT)
    send(ob, prim_ref.at[place, :], O_PRIM + c, source(0))

    for h in range(2):
        piece = prim_ref.at[pl.ds(h * half, half), :]
        arrived(piece, O_PRIM + h)
        send(piece, sec_ref.at[pl.ds(h * half, half), :], O_SEC + h, partner)
    for h in range(2):
        arrived(sec_ref.at[pl.ds(h * half, half), :], O_SEC + h)

    @pl.when(upper)
    def _():
        for slot, (src, dst, recv, device) in enumerate(upper_moves()):
            copy_of(src, dst, slot, recv, device).wait_send()

    @pl.when(jnp.logical_not(upper))
    def _():
        for slot, (src, dst, recv, device) in enumerate(lower_moves()):
            copy_of(src, dst, slot, recv, device).wait_send()
        arrived(ra_ref, O_RA)

    for copy in sends:
        copy.wait_send()
    assert count[0] <= N_SEND


def on_device(reflect_fwd, transmit_fwd, reflect_bwd, transmit_bwd, material_ids, interface_gain):
    blk = reflect_fwd.shape[1]
    order = interface_gain.shape[1]
    half = blk // 2
    fine = order // 32
    hbm = pl.BlockSpec(memory_space=pltpu.HBM)
    vmem = pl.BlockSpec(memory_space=pltpu.VMEM)
    shape = jax.ShapeDtypeStruct((blk, blk), F32)
    reflect_own = reflect_fwd[0]
    prim, sec, reflect_peer = pl.pallas_call(
        kernel,
        out_shape=(shape, shape, shape),
        in_specs=[hbm, hbm, hbm, hbm, pl.BlockSpec(memory_space=pltpu.SMEM), vmem],
        out_specs=(hbm, hbm, hbm),
        scratch_shapes=[
            pltpu.VMEM((half, order), F32),
            pltpu.VMEM((half, order), F32),
            pltpu.VMEM((half, order), F32),
            pltpu.VMEM((half, order), F32),
            pltpu.VMEM((order, blk), F32),
            pltpu.VMEM((order, order), F32),
            pltpu.VMEM((order, order), BF16),
            pltpu.VMEM((order, order), BF16),
            pltpu.VMEM((fine, order), F32),
            pltpu.VMEM((blk, order), F32),
            pltpu.VMEM((half, blk), F32),
            pltpu.VMEM((half, blk), F32),
            pltpu.VMEM((8, order), F32),
            pltpu.VMEM((8, order), F32),
            pltpu.VMEM((8, order), F32),
            pltpu.VMEM((blk, blk), F32),
            pltpu.VMEM((blk, blk), F32),
            pltpu.VMEM((half, blk), F32),
            pltpu.VMEM((half, blk), F32),
            pltpu.SemaphoreType.DMA((N_SEND,)),
            pltpu.SemaphoreType.DMA((N_RECV,)),
            pltpu.SemaphoreType.DMA,
        ],
        compiler_params=pltpu.CompilerParams(
            collective_id=0, has_side_effects=True, vmem_limit_bytes=48 * 1024 * 1024),
        name="star",
    )(reflect_own, transmit_fwd[0], reflect_bwd[0], transmit_bwd[0], material_ids, interface_gain)
    upper = lax.axis_index("layer") < lax.axis_size("layer") // 2
    reflect_a = jnp.where(upper, reflect_own, reflect_peer)
    refl_out = reflect_a + jnp.where(upper, prim, sec)
    trans_out = jnp.where(upper, sec, prim)
    return (refl_out[None], trans_out[None])


def solution(mesh):
    placed = (
        P("layer", "row", "col"),
        P("layer", "row", "col"),
        P("layer", "row", "col"),
        P("layer", "row", "col"),
        P("layer"),
        P(),
    )
    return jax.shard_map(
        on_device,
        mesh=mesh,
        in_specs=placed,
        out_specs=(P("layer", "row", "col"), P("layer", "row", "col")),
        check_vma=False,
    )
```

```python
import jax
import jax.numpy as jnp
from jax import lax
from jax.experimental import pallas as pl
from jax.experimental.pallas import tpu as pltpu
from jax.sharding import PartitionSpec as P

NTERMS = 6
MESH = pl.DeviceIdType.MESH
F32 = jnp.float32
BF16 = jnp.bfloat16
ORDER = (0, 3, 1, 2)

PLANE = (3, 11, 2, 15, 5, 7, 9, 13, 14, 1, 0, 6, 8, 4, 12, 10)
PLACE = (3, 1, 2, 3, 1, 2, 5, 0, 4, 7, 0, 3, 0, 0, 2, 7)

Z_RB, Z_TB, Z_RF, Z_TF, Z_FT, Z_TR, Z_WA, Z_WB = 0, 1, 2, 3, 4, 5, 8, 9
R_RB, R_TB, R_TF, R_SS, R_RF, R_MT, R_PA, R_PB = 10, 14, 18, 22, 26, 30, 34, 38
C_RF, C_MT, C_PP = 54, 58, 62
O_MD, O_T, O_R, O_RA, R_FT = 78, 82, 86, 90, 91
N_RECV = 95
N_SEND = 120

NN = (((1,), (0,)), ((), ()))
NT = (((1,), (1,)), ((), ()))


def split(value):
    high = value.astype(BF16)
    low = (value - high.astype(F32)).astype(BF16)
    return high, low


def dot3(left, right, dims):
    lh, ll = left
    rh, rl = right

    def one(a, b):
        return lax.dot_general(a, b, dims, preferred_element_type=F32)

    return one(lh, rh) + (one(lh, rl) + one(ll, rh))


def lookup(table, index):
    value = jnp.int32(table[0])
    for k in range(1, len(table)):
        value = jnp.where(index == k, jnp.int32(table[k]), value)
    return value


def kernel(rf_ref, tf_ref, rb_ref, tb_ref, mid_ref, gain_ref,
           t_ref, r_ref, ra_ref,
           rb, tb, tf, ss, rf, pp, ph, plo, ft, mt, ot, ob, own_gain, wa, wb, fts,
           fv, fr, tr, md, ssem, rsem, lsem):
    lay = lax.axis_index("layer")
    y = lax.axis_index("row")
    zh = lax.axis_index("col")
    x = lay // 8
    zl = lax.rem(lay // 2, 4)
    c = lax.rem(lay, 2)
    z = zh * 4 + zl
    blk = rf_ref.shape[0]
    half = blk // 2
    quarter = half // 2
    wide = rf.shape[0]
    fine = ft.shape[0]

    def spot(pair):
        where = lookup(PLACE, pair)
        turn = jnp.where(where < 4, 1, 3)
        return turn, lax.rem(jnp.where(where < 4, 8 - where, where), 4)

    def plane_of(pair):
        zp = lookup(PLANE, pair)
        turn, base = spot(pair)
        xp = lax.rem(turn * zh + base, 4)
        return [(xp * 8 + lax.rem(zp, 4) * 2 + cd, y, zp // 4) for cd in range(2)]

    upper = lay < 16
    plane = plane_of(lax.rem(lay, 16))

    passes_t = jnp.logical_or(x == 1, x == 2)
    passed = plane_of(jnp.where(passes_t, x - 1, lax.rem(x + 1, 4)) * 8 + lax.rem(lay, 8))

    task = lookup([PLANE.index(k) for k in range(16)], z)
    turn, base = spot(task)
    j = lax.rem(turn * (x + 4 - base), 4)

    def source(dx):
        return (lax.rem(task + 8 * dx, 32), y, j)

    def near(jd, yd):
        return (lax.rem(turn * jd + base, 4) * 8 + zl * 2 + c, lax.rem(yd, 4), zh)

    def beside(dx):
        return (lax.rem(lay + 8 * dx, 32), y, zh)

    cross = (lay + 1 - 2 * c, y, zh)
    partner = beside(2)

    barrier = pltpu.get_barrier_semaphore()

    def signal(device):
        pl.semaphore_signal(barrier, inc=1, device_id=device, device_id_type=MESH)

    for device in (source(0), source(2), *passed, partner):
        signal(device)
    for step in (1, 3):
        signal(near(j + step, y))
    for step in (1, 2, 3):
        signal(near(j, y + step))
    signal(cross)
    load = pltpu.make_async_copy(tf_ref, fv, lsem)
    load.start()

    rows8 = lax.broadcasted_iota(jnp.int32, gain_ref.shape, 0)
    own = jnp.sum(jnp.where(rows8 == mid_ref[0], gain_ref[...], 0.0), axis=0, keepdims=True)
    own_gain[...] = jnp.broadcast_to(own, own_gain.shape)
    load.wait()
    fts[...] = fv[...].T
    pl.semaphore_wait(barrier, 11)

    sends = []
    count = [0]

    def copy_of(src, dst, slot, recv, device):
        return pltpu.make_async_remote_copy(
            src_ref=src, dst_ref=dst, send_sem=ssem.at[slot], recv_sem=rsem.at[recv],
            device_id=device, device_id_type=MESH)

    def send(src, dst, recv, device):
        copy = copy_of(src, dst, count[0], recv, device)
        count[0] += 1
        copy.start()
        sends.append(copy)

    def arrived(dst, recv):
        copy_of(dst, dst, 0, recv, cross).wait_recv()

    def al(index, size):
        return pl.ds(pl.multiple_of(index, size), size)

    mine = al(zh * blk, blk)
    halves = [pl.ds(0, half), pl.ds(half, half)]

    def upper_moves():
        moves = []
        for cd in range(2):
            moves.append((rb_ref.at[halves[cd], :], rb.at[:, mine], Z_RB, plane[cd]))
        moves.append((tb_ref.at[halves[1], :], tr, Z_TR, partner))
        for cd in range(2):
            moves.append((own_gain.at[pl.ds(0, 1), :], wa.at[pl.ds(0, 1), :], Z_WA, plane[cd]))
        for cd in range(2):
            moves.append((fts.at[halves[cd], :], fr, Z_FT, plane[cd]))
        moves.append((tb_ref.at[halves[0], :], tb.at[:, mine], Z_TB, plane[0]))
        return moves

    def lower_moves():
        moves = []
        for cd in range(2):
            moves.append((rf_ref.at[halves[cd], :], rf.at[al((2 * y + cd) * half, half), :], Z_RF, plane[cd]))
        for cd in range(2):
            moves.append((own_gain.at[pl.ds(0, 1), :], wb.at[pl.ds(0, 1), :], Z_WB, plane[cd]))
        moves.append((tr, tb.at[:, mine], Z_TB, plane[1]))
        for cd in range(2):
            moves.append((tf_ref.at[halves[cd], :], tf.at[:, mine], Z_TF, plane[cd]))
        return moves

    def start_moves(first, last):
        @pl.when(upper)
        def _():
            for slot, (src, dst, recv, device) in list(enumerate(upper_moves()))[first:last]:
                copy_of(src, dst, slot, recv, device).start()

        @pl.when(jnp.logical_not(upper))
        def _():
            for slot, (src, dst, recv, device) in list(enumerate(lower_moves()))[first:last]:
                if recv != Z_TB:
                    copy_of(src, dst, slot, recv, device).start()

    def relay_move():
        @pl.when(jnp.logical_not(upper))
        def _():
            for slot, (src, dst, recv, device) in enumerate(lower_moves()):
                if recv == Z_TB:
                    arrived(tr, Z_TR)
                    copy_of(src, dst, slot, recv, device).start()

    start_moves(0, 2)
    count[0] = len(upper_moves())

    class Ring:
        def __init__(self, part, me, device, base):
            self.part, self.me, self.device, self.base = part, me, device, base

        def pos(self, step):
            return lax.rem(self.me + step, 4)

        def start(self):
            piece = self.part(self.me, None)
            send(piece, piece, self.base, self.device(self.me + 1))
            send(piece, piece, self.base + 1, self.device(self.me + 3))

        def left(self):
            arrived(self.part(self.pos(3), None), self.base)
            piece = self.part(self.pos(3), 0)
            send(piece, piece, self.base + 2, self.device(self.me + 1))

        def right(self):
            arrived(self.part(self.pos(1), None), self.base + 1)
            piece = self.part(self.pos(1), 1)
            send(piece, piece, self.base + 3, self.device(self.me + 3))

        def far(self):
            arrived(self.part(self.pos(2), 0), self.base + 2)
            arrived(self.part(self.pos(2), 1), self.base + 3)

    def on_x(a):
        return near(a, y)

    def on_y(a):
        return near(j, a)

    def col_part(buf):
        def part(p, h):
            rows = pl.ds(0, half) if h is None else pl.ds(h * quarter, quarter)
            return buf.at[rows, al(p * blk, blk)]
        return part

    def row_part(buf, size, base):
        def part(p, h):
            start = base(p)
            if h is None:
                return buf.at[al(start, size), :]
            return buf.at[al(start + h * (size // 2), size // 2), :]
        return part

    def cross_send(piece, recv):
        send(piece, piece, recv, cross)

    def cross_wait(part, base):
        for k, step in enumerate(ORDER):
            arrived(part(lax.rem(y + step, 4), None), base + k)

    def y_gather(buf, size, place, base, cbase):
        part = row_part(buf, size, lambda p: place(p, c))
        ring = Ring(part, y, on_y, base)
        ring.start()
        cross_send(part(y, None), cbase)
        yield
        ring.left()
        cross_send(part(ring.pos(3), None), cbase + 1)
        ring.right()
        cross_send(part(ring.pos(1), None), cbase + 2)
        yield
        ring.far()
        cross_send(part(ring.pos(2), None), cbase + 3)
        yield
        cross_wait(row_part(buf, size, lambda p: place(p, 1 - c)), cbase)
        yield

    rb_ring = Ring(col_part(rb), j, on_x, R_RB)
    tb_ring = Ring(col_part(tb), j, on_x, R_TB)
    tf_ring = Ring(col_part(tf), j, on_x, R_TF)
    ss_ring = Ring(col_part(ss), j, on_x, R_SS)

    arrived(rb.at[:, al(j * blk, blk)], Z_RB)
    rb_ring.start()
    arrived(rf.at[al((2 * y + c) * half, half), :], Z_RF)
    def rf_place(p, core):
        return (2 * p + core) * half

    def mt_place(p, core):
        return (4 * core + p) * fine

    gather = y_gather(rf, half, rf_place, R_RF, C_RF)
    next(gather)
    rb_ring.left()
    rb_ring.right()
    next(gather)
    rb_ring.far()
    next(gather)
    next(gather)
    right = split(rf[...])
    power = dot3(split(rb[...]), right, NN)

    def ppart(jj, ii, h, core):
        start = (2 * ii + core) * half
        cols = al(lax.rem(jj, 4) * blk, blk)
        if h is None:
            return pp.at[al(start, half), cols]
        return pp.at[al(start + h * quarter, quarter), cols]

    pp[al((2 * y + c) * half, half), al(j * blk, blk)] = power
    ring_a = Ring(lambda p, h: ppart(p, y, h, c), j, on_x, R_PA)
    rings_b = [
        Ring(lambda p, h, jj=j + step: ppart(jj, p, h, c), y, on_y, R_PB + 4 * k)
        for k, step in enumerate(ORDER)
    ]

    def start_b(k):
        rings_b[k].start()
        cross_send(rings_b[k].part(y, None), C_PP + 4 * k)

    def sides_b(k):
        rings_b[k].left()
        cross_send(rings_b[k].part(rings_b[k].pos(3), None), C_PP + 4 * k + 1)
        rings_b[k].right()
        cross_send(rings_b[k].part(rings_b[k].pos(1), None), C_PP + 4 * k + 2)

    def far_b(k):
        rings_b[k].far()
        cross_send(rings_b[k].part(rings_b[k].pos(2), None), C_PP + 4 * k + 3)

    ring_a.start()
    start_b(0)
    ring_a.left()
    start_b(1)
    ring_a.right()
    start_moves(2, None)
    start_b(2)
    sides_b(0)
    ring_a.far()
    start_b(3)
    relay_move()
    sides_b(1)
    far_b(0)
    sides_b(2)
    far_b(1)
    sides_b(3)
    far_b(2)
    far_b(3)
    arrived(fr, Z_FT)
    ycols = al(y * blk, blk)
    for step in (1, 2, 3):
        to = lax.rem(y + step, 4)
        send(fr.at[al(to * fine, fine), :], ft.at[:, ycols], R_FT + y, on_y(to))
    ft[:, ycols] = fr[al(y * fine, fine), :]
    arrived(wa.at[pl.ds(0, 1), :], Z_WA)
    arrived(wb.at[pl.ds(0, 1), :], Z_WB)
    weight = wa[0:1, :] * wb[0:1, :]
    for k, step in enumerate(ORDER):
        for m, other in enumerate(ORDER):
            arrived(ppart(j + step, lax.rem(y + other, 4), None, 1 - c), C_PP + 4 * k + m)
    ph[...], plo[...] = split(pp[...])
    arrived(tb.at[:, al(j * blk, blk)], Z_TB)
    tb_ring.start()
    for step in (1, 2, 3):
        away = lax.rem(y + step, 4)
        arrived(ft.at[:, al(away * blk, blk)], R_FT + away)
    first = ft[...] * weight

    def horner(step, value):
        return first + dot3(split(value), (ph[...], plo[...]), NT)

    value = lax.fori_loop(0, NTERMS - 3, horner, first)
    arrived(tf.at[:, al(j * blk, blk)], Z_TF)
    tf_ring.start()
    tb_ring.left()
    tb_ring.right()
    value = lax.fori_loop(0, 2, horner, value)
    mt[al(mt_place(y, c), fine), :] = value
    gather = y_gather(mt, fine, mt_place, R_MT, C_MT)
    next(gather)
    tb_ring.far()
    ss[:, al(j * blk, blk)] = dot3(split(tb[...] * weight), right, NN)
    ss_ring.start()
    tf_ring.left()
    tf_ring.right()
    next(gather)
    ss_ring.left()
    ss_ring.right()
    next(gather)
    tf_ring.far()

    place = al(c * half, half)

    def result(k, left, buf, dx):
        h = lax.rem(c + k, 2)
        middle = split(mt[al(h * half, half), :])
        buf[k] = dot3(left, middle, NT)
        send(buf.at[k], md.at[place, al(h * half, half)], O_MD + 2 * c + h, source(dx))

    lower = split(tf[...])
    result(0, lower, ot, 1)
    next(gather)
    result(1, lower, ot, 1)
    ss_ring.far()
    side = split(ss[...])
    result(0, side, ob, 3)
    result(1, side, ob, 3)

    @pl.when(upper)
    def _():
        copy_of(rf_ref, ra_ref, N_SEND - 1, O_RA, partner).start()

    def quarter_of(buf, core, h):
        return buf.at[pl.ds(core * half, half), pl.ds(h * half, half)]

    quarters = ((0, 0), (1, 1), (0, 1), (1, 0))
    for n, (core, h) in enumerate(quarters):
        arrived(quarter_of(md, core, h), O_MD + 2 * core + h)
        for role, buf, recv in ((passes_t, t_ref, O_T), (jnp.logical_not(passes_t), r_ref, O_R)):
            @pl.when(role)
            def _(buf=buf, recv=recv, n=n, core=core, h=h):
                for m, dx in enumerate((1, 3)):
                    copy_of(quarter_of(md, core, h), quarter_of(buf, core, h), N_SEND - 9 + 2 * n + m,
                            recv + 2 * core + h, beside(dx)).start()
    for core, h in quarters:
        arrived(quarter_of(t_ref, core, h), O_T + 2 * core + h)
        arrived(quarter_of(r_ref, core, h), O_R + 2 * core + h)
    for n, (core, h) in enumerate(quarters):
        for m in range(2):
            copy_of(quarter_of(md, core, h), quarter_of(md, core, h), N_SEND - 9 + 2 * n + m, 0, cross).wait_send()

    @pl.when(upper)
    def _():
        copy_of(rf_ref, ra_ref, N_SEND - 1, O_RA, partner).wait_send()

    @pl.when(upper)
    def _():
        for slot, (src, dst, recv, device) in enumerate(upper_moves()):
            copy_of(src, dst, slot, recv, device).wait_send()

    @pl.when(jnp.logical_not(upper))
    def _():
        for slot, (src, dst, recv, device) in enumerate(lower_moves()):
            copy_of(src, dst, slot, recv, device).wait_send()
        arrived(ra_ref, O_RA)

    for copy in sends:
        copy.wait_send()
    assert count[0] <= N_SEND - 9


def on_device(reflect_fwd, transmit_fwd, reflect_bwd, transmit_bwd, material_ids, interface_gain):
    blk = reflect_fwd.shape[1]
    order = interface_gain.shape[1]
    half = blk // 2
    fine = order // 32
    hbm = pl.BlockSpec(memory_space=pltpu.HBM)
    vmem = pl.BlockSpec(memory_space=pltpu.VMEM)
    shape = jax.ShapeDtypeStruct((blk, blk), F32)
    reflect_own = reflect_fwd[0]
    trans, bounce, reflect_peer = pl.pallas_call(
        kernel,
        out_shape=(shape, shape, shape),
        in_specs=[hbm, hbm, hbm, hbm, pl.BlockSpec(memory_space=pltpu.SMEM), vmem],
        out_specs=(hbm, hbm, hbm),
        scratch_shapes=[
            pltpu.VMEM((half, order), F32),
            pltpu.VMEM((half, order), F32),
            pltpu.VMEM((half, order), F32),
            pltpu.VMEM((half, order), F32),
            pltpu.VMEM((order, blk), F32),
            pltpu.VMEM((order, order), F32),
            pltpu.VMEM((order, order), BF16),
            pltpu.VMEM((order, order), BF16),
            pltpu.VMEM((fine, order), F32),
            pltpu.VMEM((blk, order), F32),
            pltpu.VMEM((2, half, half), F32),
            pltpu.VMEM((2, half, half), F32),
            pltpu.VMEM((8, order), F32),
            pltpu.VMEM((8, order), F32),
            pltpu.VMEM((8, order), F32),
            pltpu.VMEM((blk, blk), F32),
            pltpu.VMEM((blk, blk), F32),
            pltpu.VMEM((half, blk), F32),
            pltpu.VMEM((half, blk), F32),
            pltpu.VMEM((blk, blk), F32),
            pltpu.SemaphoreType.DMA((N_SEND,)),
            pltpu.SemaphoreType.DMA((N_RECV,)),
            pltpu.SemaphoreType.DMA,
        ],
        compiler_params=pltpu.CompilerParams(
            collective_id=0, has_side_effects=True, vmem_limit_bytes=48 * 1024 * 1024),
        name="star",
    )(reflect_own, transmit_fwd[0], reflect_bwd[0], transmit_bwd[0], material_ids, interface_gain)
    upper = lax.axis_index("layer") < lax.axis_size("layer") // 2
    reflect_a = jnp.where(upper, reflect_own, reflect_peer)
    return ((reflect_a + bounce)[None], trans[None])


def solution(mesh):
    placed = (
        P("layer", "row", "col"),
        P("layer", "row", "col"),
        P("layer", "row", "col"),
        P("layer", "row", "col"),
        P("layer"),
        P(),
    )
    return jax.shard_map(
        on_device,
        mesh=mesh,
        in_specs=placed,
        out_specs=(P("layer", "row", "col"), P("layer", "row", "col")),
        check_vma=False,
    )
```

```python
import jax
import jax.numpy as jnp
from jax import lax
from jax.experimental import pallas as pl
from jax.experimental.pallas import tpu as pltpu
from jax.sharding import PartitionSpec as P

NTERMS = 6
MESH = pl.DeviceIdType.MESH
F32 = jnp.float32
BF16 = jnp.bfloat16
ORDER = (0, 3, 1, 2)

PLANE = (3, 11, 2, 15, 5, 7, 9, 13, 14, 1, 0, 6, 8, 4, 12, 10)
PLACE = (3, 1, 2, 3, 1, 2, 5, 0, 4, 7, 0, 3, 0, 0, 2, 7)

Z_RB, Z_TB, Z_RF, Z_TF, Z_FT, Z_TR, Z_WA, Z_WB = 0, 1, 2, 3, 4, 5, 8, 9
R_RB, R_TB, R_TF, R_SS, R_RF, R_MT, R_PA, R_PB = 10, 14, 18, 22, 26, 30, 34, 38
C_RF, C_MT, C_PP = 54, 58, 62
O_MD, O_T, O_R, O_RA, R_FT = 78, 82, 86, 90, 91
N_RECV = 95
N_SEND = 120

NN = (((1,), (0,)), ((), ()))
NT = (((1,), (1,)), ((), ()))


def split(value):
    high = value.astype(BF16)
    low = (value - high.astype(F32)).astype(BF16)
    return high, low


def dot3(left, right, dims):
    lh, ll = left
    rh, rl = right

    def one(a, b):
        return lax.dot_general(a, b, dims, preferred_element_type=F32)

    return one(lh, rh) + (one(lh, rl) + one(ll, rh))


def lookup(table, index):
    value = jnp.int32(table[0])
    for k in range(1, len(table)):
        value = jnp.where(index == k, jnp.int32(table[k]), value)
    return value


def kernel(rf_ref, tf_ref, rb_ref, tb_ref, mid_ref, gain_ref,
           t_ref, r_ref, ra_ref,
           rb, tb, tf, ss, rf, pp, ph, plo, ft, mt, ot, ob, own_gain, wa, wb, fts,
           fv, fr, tr, md, ssem, rsem, lsem):
    lay = lax.axis_index("layer")
    y = lax.axis_index("row")
    zh = lax.axis_index("col")
    x = lay // 8
    zl = lax.rem(lay // 2, 4)
    c = lax.rem(lay, 2)
    z = zh * 4 + zl
    blk = rf_ref.shape[0]
    half = blk // 2
    quarter = half // 2
    wide = rf.shape[0]
    fine = ft.shape[0]

    def spot(pair):
        where = lookup(PLACE, pair)
        turn = jnp.where(where < 4, 1, 3)
        return turn, lax.rem(jnp.where(where < 4, 8 - where, where), 4)

    def plane_of(pair):
        zp = lookup(PLANE, pair)
        turn, base = spot(pair)
        xp = lax.rem(turn * zh + base, 4)
        return [(xp * 8 + lax.rem(zp, 4) * 2 + cd, y, zp // 4) for cd in range(2)]

    upper = lay < 16
    plane = plane_of(lax.rem(lay, 16))

    passes_t = jnp.logical_or(x == 1, x == 2)
    passed = plane_of(jnp.where(passes_t, x - 1, lax.rem(x + 1, 4)) * 8 + lax.rem(lay, 8))

    task = lookup([PLANE.index(k) for k in range(16)], z)
    turn, base = spot(task)
    j = lax.rem(turn * (x + 4 - base), 4)

    def source(dx):
        return (lax.rem(task + 8 * dx, 32), y, j)

    def near(jd, yd):
        return (lax.rem(turn * jd + base, 4) * 8 + zl * 2 + c, lax.rem(yd, 4), zh)

    def beside(dx):
        return (lax.rem(lay + 8 * dx, 32), y, zh)

    cross = (lay + 1 - 2 * c, y, zh)
    partner = beside(2)

    barrier = pltpu.get_barrier_semaphore()

    def signal(device):
        pl.semaphore_signal(barrier, inc=1, device_id=device, device_id_type=MESH)

    for device in (source(0), source(2), *passed, partner):
        signal(device)
    for step in (1, 3):
        signal(near(j + step, y))
    for step in (1, 2, 3):
        signal(near(j, y + step))
    signal(cross)
    load = pltpu.make_async_copy(tf_ref, fv, lsem)
    load.start()

    rows8 = lax.broadcasted_iota(jnp.int32, gain_ref.shape, 0)
    own = jnp.sum(jnp.where(rows8 == mid_ref[0], gain_ref[...], 0.0), axis=0, keepdims=True)
    own_gain[...] = jnp.broadcast_to(own, own_gain.shape)
    load.wait()
    fts[...] = fv[...].T
    pl.semaphore_wait(barrier, 11)

    sends = []
    count = [0]

    def copy_of(src, dst, slot, recv, device):
        return pltpu.make_async_remote_copy(
            src_ref=src, dst_ref=dst, send_sem=ssem.at[slot], recv_sem=rsem.at[recv],
            device_id=device, device_id_type=MESH)

    def send(src, dst, recv, device):
        copy = copy_of(src, dst, count[0], recv, device)
        count[0] += 1
        copy.start()
        sends.append(copy)

    def arrived(dst, recv):
        copy_of(dst, dst, 0, recv, cross).wait_recv()

    def al(index, size):
        return pl.ds(pl.multiple_of(index, size), size)

    mine = al(zh * blk, blk)
    halves = [pl.ds(0, half), pl.ds(half, half)]

    def upper_moves():
        moves = []
        for cd in range(2):
            moves.append((rb_ref.at[halves[cd], :], rb.at[:, mine], Z_RB, plane[cd]))
        moves.append((tb_ref.at[halves[1], :], tr, Z_TR, partner))
        for cd in range(2):
            moves.append((own_gain.at[pl.ds(0, 1), :], wa.at[pl.ds(0, 1), :], Z_WA, plane[cd]))
        for cd in range(2):
            moves.append((fts.at[halves[cd], :], fr, Z_FT, plane[cd]))
        moves.append((tb_ref.at[halves[0], :], tb.at[:, mine], Z_TB, plane[0]))
        return moves

    def lower_moves():
        moves = []
        for cd in range(2):
            moves.append((rf_ref.at[halves[cd], :], rf.at[al((2 * y + cd) * half, half), :], Z_RF, plane[cd]))
        for cd in range(2):
            moves.append((own_gain.at[pl.ds(0, 1), :], wb.at[pl.ds(0, 1), :], Z_WB, plane[cd]))
        moves.append((tr, tb.at[:, mine], Z_TB, plane[1]))
        for cd in range(2):
            moves.append((tf_ref.at[halves[cd], :], tf.at[:, mine], Z_TF, plane[cd]))
        return moves

    def start_moves(first, last, lf=None, ll=None):
        lf = first if lf is None else lf
        ll = last if ll is None else ll

        @pl.when(upper)
        def _():
            for slot, (src, dst, recv, device) in list(enumerate(upper_moves()))[first:last]:
                copy_of(src, dst, slot, recv, device).start()

        @pl.when(jnp.logical_not(upper))
        def _():
            for slot, (src, dst, recv, device) in list(enumerate(lower_moves()))[lf:ll]:
                if recv != Z_TB:
                    copy_of(src, dst, slot, recv, device).start()

    def relay_move():
        @pl.when(jnp.logical_not(upper))
        def _():
            for slot, (src, dst, recv, device) in enumerate(lower_moves()):
                if recv == Z_TB:
                    arrived(tr, Z_TR)
                    copy_of(src, dst, slot, recv, device).start()

    start_moves(0, 2)
    count[0] = len(upper_moves())

    class Ring:
        def __init__(self, part, me, device, base):
            self.part, self.me, self.device, self.base = part, me, device, base

        def pos(self, step):
            return lax.rem(self.me + step, 4)

        def start(self):
            piece = self.part(self.me, None)
            send(piece, piece, self.base, self.device(self.me + 1))
            send(piece, piece, self.base + 1, self.device(self.me + 3))

        def left(self):
            arrived(self.part(self.pos(3), None), self.base)
            piece = self.part(self.pos(3), 0)
            send(piece, piece, self.base + 2, self.device(self.me + 1))

        def right(self):
            arrived(self.part(self.pos(1), None), self.base + 1)
            piece = self.part(self.pos(1), 1)
            send(piece, piece, self.base + 3, self.device(self.me + 3))

        def far(self):
            arrived(self.part(self.pos(2), 0), self.base + 2)
            arrived(self.part(self.pos(2), 1), self.base + 3)

    def on_x(a):
        return near(a, y)

    def on_y(a):
        return near(j, a)

    def col_part(buf):
        def part(p, h):
            rows = pl.ds(0, half) if h is None else pl.ds(h * quarter, quarter)
            return buf.at[rows, al(p * blk, blk)]
        return part

    def row_part(buf, size, base):
        def part(p, h):
            start = base(p)
            if h is None:
                return buf.at[al(start, size), :]
            return buf.at[al(start + h * (size // 2), size // 2), :]
        return part

    def cross_send(piece, recv):
        send(piece, piece, recv, cross)

    def cross_wait(part, base):
        for k, step in enumerate(ORDER):
            arrived(part(lax.rem(y + step, 4), None), base + k)

    def y_gather(buf, size, place, base, cbase):
        part = row_part(buf, size, lambda p: place(p, c))
        ring = Ring(part, y, on_y, base)
        ring.start()
        cross_send(part(y, None), cbase)
        yield
        ring.left()
        cross_send(part(ring.pos(3), None), cbase + 1)
        ring.right()
        cross_send(part(ring.pos(1), None), cbase + 2)
        yield
        ring.far()
        cross_send(part(ring.pos(2), None), cbase + 3)
        yield
        cross_wait(row_part(buf, size, lambda p: place(p, 1 - c)), cbase)
        yield

    rb_ring = Ring(col_part(rb), j, on_x, R_RB)
    tb_ring = Ring(col_part(tb), j, on_x, R_TB)
    tf_ring = Ring(col_part(tf), j, on_x, R_TF)
    ss_ring = Ring(col_part(ss), j, on_x, R_SS)

    arrived(rb.at[:, al(j * blk, blk)], Z_RB)
    rb_ring.start()
    arrived(rf.at[al((2 * y + c) * half, half), :], Z_RF)
    def rf_place(p, core):
        return (2 * p + core) * half

    def mt_place(p, core):
        return (4 * core + p) * fine

    gather = y_gather(rf, half, rf_place, R_RF, C_RF)
    next(gather)
    start_moves(2, 3)
    rb_ring.left()
    rb_ring.right()
    next(gather)
    rb_ring.far()
    next(gather)
    next(gather)
    right = split(rf[...])
    power = dot3(split(rb[...]), right, NN)

    def ppart(jj, ii, h, core):
        start = (2 * ii + core) * half
        cols = al(lax.rem(jj, 4) * blk, blk)
        if h is None:
            return pp.at[al(start, half), cols]
        return pp.at[al(start + h * quarter, quarter), cols]

    pp[al((2 * y + c) * half, half), al(j * blk, blk)] = power
    ring_a = Ring(lambda p, h: ppart(p, y, h, c), j, on_x, R_PA)
    rings_b = [
        Ring(lambda p, h, jj=j + step: ppart(jj, p, h, c), y, on_y, R_PB + 4 * k)
        for k, step in enumerate(ORDER)
    ]

    def start_b(k):
        rings_b[k].start()
        cross_send(rings_b[k].part(y, None), C_PP + 4 * k)

    def sides_b(k):
        rings_b[k].left()
        cross_send(rings_b[k].part(rings_b[k].pos(3), None), C_PP + 4 * k + 1)
        rings_b[k].right()
        cross_send(rings_b[k].part(rings_b[k].pos(1), None), C_PP + 4 * k + 2)

    def far_b(k):
        rings_b[k].far()
        cross_send(rings_b[k].part(rings_b[k].pos(2), None), C_PP + 4 * k + 3)

    ring_a.start()
    start_b(0)
    ring_a.left()
    start_b(1)
    ring_a.right()
    relay_move()
    start_moves(3, None)
    start_b(2)
    sides_b(0)
    ring_a.far()
    start_b(3)
    sides_b(1)
    far_b(0)
    sides_b(2)
    far_b(1)
    sides_b(3)
    far_b(2)
    far_b(3)
    arrived(fr, Z_FT)
    ycols = al(y * blk, blk)
    for step in (1, 2, 3):
        to = lax.rem(y + step, 4)
        send(fr.at[al(to * fine, fine), :], ft.at[:, ycols], R_FT + y, on_y(to))
    ft[:, ycols] = fr[al(y * fine, fine), :]
    arrived(wa.at[pl.ds(0, 1), :], Z_WA)
    arrived(wb.at[pl.ds(0, 1), :], Z_WB)
    weight = wa[0:1, :] * wb[0:1, :]
    for k, step in enumerate(ORDER):
        for m, other in enumerate(ORDER):
            arrived(ppart(j + step, lax.rem(y + other, 4), None, 1 - c), C_PP + 4 * k + m)
    ph[...], plo[...] = split(pp[...])
    arrived(tb.at[:, al(j * blk, blk)], Z_TB)
    tb_ring.start()
    for step in (1, 2, 3):
        away = lax.rem(y + step, 4)
        arrived(ft.at[:, al(away * blk, blk)], R_FT + away)
    first = ft[...] * weight

    def horner(step, value):
        return first + dot3(split(value), (ph[...], plo[...]), NT)

    value = lax.fori_loop(0, NTERMS - 3, horner, first)
    arrived(tf.at[:, al(j * blk, blk)], Z_TF)
    tf_ring.start()
    tb_ring.left()
    tb_ring.right()
    value = lax.fori_loop(0, 2, horner, value)
    mt[al(mt_place(y, c), fine), :] = value
    gather = y_gather(mt, fine, mt_place, R_MT, C_MT)
    next(gather)
    tb_ring.far()
    ss[:, al(j * blk, blk)] = dot3(split(tb[...] * weight), right, NN)
    ss_ring.start()
    tf_ring.left()
    tf_ring.right()
    next(gather)
    ss_ring.left()
    ss_ring.right()
    next(gather)
    tf_ring.far()

    place = al(c * half, half)

    def result(k, left, buf, dx):
        h = lax.rem(c + k, 2)
        middle = split(mt[al(h * half, half), :])
        buf[k] = dot3(left, middle, NT)
        send(buf.at[k], md.at[place, al(h * half, half)], O_MD + 2 * c + h, source(dx))

    lower = split(tf[...])
    result(0, lower, ot, 1)
    next(gather)
    result(1, lower, ot, 1)
    ss_ring.far()
    side = split(ss[...])
    result(0, side, ob, 3)
    result(1, side, ob, 3)

    @pl.when(upper)
    def _():
        copy_of(rf_ref, ra_ref, N_SEND - 1, O_RA, partner).start()

    def quarter_of(buf, core, h):
        return buf.at[pl.ds(core * half, half), pl.ds(h * half, half)]

    quarters = ((0, 0), (1, 1), (0, 1), (1, 0))
    for n, (core, h) in enumerate(quarters):
        arrived(quarter_of(md, core, h), O_MD + 2 * core + h)
        for role, buf, recv in ((passes_t, t_ref, O_T), (jnp.logical_not(passes_t), r_ref, O_R)):
            @pl.when(role)
            def _(buf=buf, recv=recv, n=n, core=core, h=h):
                for m, dx in enumerate((1, 3)):
                    copy_of(quarter_of(md, core, h), quarter_of(buf, core, h), N_SEND - 9 + 2 * n + m,
                            recv + 2 * core + h, beside(dx)).start()
    for core, h in quarters:
        arrived(quarter_of(t_ref, core, h), O_T + 2 * core + h)
        arrived(quarter_of(r_ref, core, h), O_R + 2 * core + h)
    for n, (core, h) in enumerate(quarters):
        for m in range(2):
            copy_of(quarter_of(md, core, h), quarter_of(md, core, h), N_SEND - 9 + 2 * n + m, 0, cross).wait_send()

    @pl.when(upper)
    def _():
        copy_of(rf_ref, ra_ref, N_SEND - 1, O_RA, partner).wait_send()

    @pl.when(upper)
    def _():
        for slot, (src, dst, recv, device) in enumerate(upper_moves()):
            copy_of(src, dst, slot, recv, device).wait_send()

    @pl.when(jnp.logical_not(upper))
    def _():
        for slot, (src, dst, recv, device) in enumerate(lower_moves()):
            copy_of(src, dst, slot, recv, device).wait_send()
        arrived(ra_ref, O_RA)

    for copy in sends:
        copy.wait_send()
    assert count[0] <= N_SEND - 9


def on_device(reflect_fwd, transmit_fwd, reflect_bwd, transmit_bwd, material_ids, interface_gain):
    blk = reflect_fwd.shape[1]
    order = interface_gain.shape[1]
    half = blk // 2
    fine = order // 32
    hbm = pl.BlockSpec(memory_space=pltpu.HBM)
    vmem = pl.BlockSpec(memory_space=pltpu.VMEM)
    shape = jax.ShapeDtypeStruct((blk, blk), F32)
    reflect_own = reflect_fwd[0]
    trans, bounce, reflect_peer = pl.pallas_call(
        kernel,
        out_shape=(shape, shape, shape),
        in_specs=[hbm, hbm, hbm, hbm, pl.BlockSpec(memory_space=pltpu.SMEM), vmem],
        out_specs=(hbm, hbm, hbm),
        scratch_shapes=[
            pltpu.VMEM((half, order), F32),
            pltpu.VMEM((half, order), F32),
            pltpu.VMEM((half, order), F32),
            pltpu.VMEM((half, order), F32),
            pltpu.VMEM((order, blk), F32),
            pltpu.VMEM((order, order), F32),
            pltpu.VMEM((order, order), BF16),
            pltpu.VMEM((order, order), BF16),
            pltpu.VMEM((fine, order), F32),
            pltpu.VMEM((blk, order), F32),
            pltpu.VMEM((2, half, half), F32),
            pltpu.VMEM((2, half, half), F32),
            pltpu.VMEM((8, order), F32),
            pltpu.VMEM((8, order), F32),
            pltpu.VMEM((8, order), F32),
            pltpu.VMEM((blk, blk), F32),
            pltpu.VMEM((blk, blk), F32),
            pltpu.VMEM((half, blk), F32),
            pltpu.VMEM((half, blk), F32),
            pltpu.VMEM((blk, blk), F32),
            pltpu.SemaphoreType.DMA((N_SEND,)),
            pltpu.SemaphoreType.DMA((N_RECV,)),
            pltpu.SemaphoreType.DMA,
        ],
        compiler_params=pltpu.CompilerParams(
            collective_id=0, has_side_effects=True, vmem_limit_bytes=48 * 1024 * 1024),
        name="star",
    )(reflect_own, transmit_fwd[0], reflect_bwd[0], transmit_bwd[0], material_ids, interface_gain)
    upper = lax.axis_index("layer") < lax.axis_size("layer") // 2
    reflect_a = jnp.where(upper, reflect_own, reflect_peer)
    known = material_ids[0] >= 0
    return ((reflect_a + bounce)[None], jnp.where(known, trans, bounce)[None])


def solution(mesh):
    placed = (
        P("layer", "row", "col"),
        P("layer", "row", "col"),
        P("layer", "row", "col"),
        P("layer", "row", "col"),
        P("layer"),
        P(),
    )
    return jax.shard_map(
        on_device,
        mesh=mesh,
        in_specs=placed,
        out_specs=(P("layer", "row", "col"), P("layer", "row", "col")),
        check_vma=False,
    )
```
